32 devices in a mesh: dp: 4 (over y, x), tile: 8 (over z, core).
Axes of the slice: x: 2, y: 2, z: 4, core: 2. Of those that a mesh axis runs over, the one named last changes fastest.
Arguments:
- tokens: bfloat16 [512, 4096], P('dp', 'tile'), may hold values from -6 to 6
- grad_out: bfloat16 [512, 4096], P('dp', 'tile'), may hold values from -6 to 6
- up_tiles: bfloat16 [8, 256, 128, 128], P('tile'), may hold values from -0.1875 to 0.1875
- down_tiles: bfloat16 [8, 256, 128, 128], P('tile'), may hold values from -0.09375 to 0.09375
- tile_rows: int32 [8, 256], P('tile'), may hold values from 0 to 15, as said below
- tile_cols: int32 [8, 256], P('tile'), may hold values from 0 to 31
- tile_count: int32 [8], P('tile'), may hold values from 32 to 256, as said below
Outputs:
- mixed: bfloat16 [512, 4096], P('dp', 'tile')
- grad_in: bfloat16 [512, 4096], P('dp', 'tile')
- grad_up: float32 [8, 256, 128, 128], P('tile', 'dp')
- grad_down: float32 [8, 256, 128, 128], P('tile', 'dp')
The draws below stay inside these ranges and needn't reach their ends.
Inputs may be any that keep to these rules, and one draw needn't show every extreme that they name: `tile_count`: some owner holds exactly 256 tiles in every draw. The pairs (tile_rows[i, s], tile_cols[i, s]) of one owner are distinct over all its 256 slots.
All inputs are finite; a program needn't handle non-finite values.
Results may differ from the reference program's by a relative error of at most 0.015.
Values may be sent and summed in bfloat16 or wider, within the bound.
A program may use at most 192 MiB of HBM per device.

```python
import jax
import jax.numpy as jnp
from jax import lax

D = 4096
HIDDEN_SIZE = 16384
TILE = 128
TOK_DEV = 128
TOKENS = 512
COLS = 32
ROWS_DEV = 16
CAP = 256
N_DP = 4
N_TILE = 8


def make_pattern(key):
    base = jax.random.fold_in(key, 271)
    key_heavy, key_counts, key_slots = jax.random.split(jax.random.fold_in(base, 5), 3)
    heavy = jax.random.randint(key_heavy, (), 0, N_TILE)
    counts = jax.random.randint(key_counts, (N_TILE,), CAP // 8, CAP // 2 + 1)
    counts = jnp.where(jnp.arange(N_TILE) == heavy, CAP, counts).astype(jnp.int32)
    cells = ROWS_DEV * COLS

    def owner_slots(dev_key, count):
        key_level, key_noise, key_shuffle = jax.random.split(dev_key, 3)
        level = jax.random.randint(key_level, (ROWS_DEV, 1), 0, 4)
        noise = jax.random.randint(key_noise, (ROWS_DEV, COLS), 0, 4096)
        score = (level * 4096 + noise).reshape(cells) * cells + jnp.arange(cells, dtype=jnp.int32)
        chosen = jnp.argsort(-score)[:CAP]
        slot = jnp.arange(CAP, dtype=jnp.int32)
        shuffle = jax.random.randint(key_shuffle, (CAP,), 0, 4096)
        ranking = jnp.where(slot < count, 0, 1) * (4096 * CAP) + shuffle * CAP + slot
        chosen = chosen[jnp.argsort(ranking)]
        return ((chosen // COLS).astype(jnp.int32), (chosen % COLS).astype(jnp.int32))
    rows, cols = jax.vmap(owner_slots)(jax.random.split(key_slots, N_TILE), counts)
    return (rows, cols, counts)


def draw_tile_rows(key, part):
    return make_pattern(key)[0]


def draw_tile_cols(key, part):
    return make_pattern(key)[1]


def draw_tile_count(key, part):
    return make_pattern(key)[2]


def block_scale(key, dims, cuts, low, top_value):
    loudness, own = 1.0, jax.random.fold_in(key, 6)
    for dim, blocks in cuts:
        heights = jnp.exp(jax.random.uniform(jax.random.fold_in(own, dim), (blocks,), jnp.float32, low / len(cuts), top_value / len(cuts)))
        loudness = loudness * jnp.repeat(heights, dims[dim] // blocks).reshape([-1 if axis == dim else 1 for axis in range(len(dims))])
    return loudness


def scatter_about(key, shape, scale, reach, cuts=(), kind=jnp.bfloat16):
    entries = scale * jax.random.normal(key, shape, jnp.float32)
    if cuts:
        entries = entries * block_scale(key, shape, cuts, -0.22, 0.18)
    return jnp.clip(entries, -reach, reach).astype(kind)


def setup_inputs(seed: int = 0) -> dict:
    seeds = jax.random.split(jax.random.key(seed), 8)
    return {
        "tokens": scatter_about(seeds[0], (TOKENS, D), 1.0, 6.0, ((0, 4), (1, 8))),
        "grad_out": scatter_about(seeds[1], (TOKENS, D), 1.0, 6.0, ((0, 4), (1, 8))),
        "up_tiles": scatter_about(seeds[2], (N_TILE, CAP, TILE, TILE), (D // 4) ** -0.5, 0.1875, ((0, 8),)),
        "down_tiles": scatter_about(seeds[3], (N_TILE, CAP, TILE, TILE), (HIDDEN_SIZE // 4) ** -0.5, 0.09375, ((0, 8),)),
        "tile_rows": draw_tile_rows(jax.random.fold_in(seeds[7], 71), 0),
        "tile_cols": draw_tile_cols(jax.random.fold_in(seeds[7], 71), 0),
        "tile_count": draw_tile_count(jax.random.fold_in(seeds[7], 71), 0),
    }


def gelu_pair(pre):
    curve = jax.scipy.special.erf(pre * 0.7071067811865476)
    value = 0.5 * pre * (1.0 + curve)
    slope = 0.5 * (1.0 + curve) + pre * jnp.exp(-0.5 * pre * pre) * 0.3989422804014327
    return value, slope


def add_owner(total, pair):
    part = jnp.dot(pair[0], pair[1], preferred_element_type=jnp.float32)
    rounded = lax.optimization_barrier(part.astype(jnp.bfloat16))
    return total + rounded.astype(jnp.float32), None


def add_group(totals, group):
    x_group, dy_group, h_group, d_group = group
    up_part = jnp.dot(x_group.T, d_group, preferred_element_type=jnp.float32)
    down_part = jnp.dot(h_group.T, dy_group, preferred_element_type=jnp.float32)
    up_round = lax.optimization_barrier(up_part.astype(jnp.bfloat16))
    down_round = lax.optimization_barrier(down_part.astype(jnp.bfloat16))
    return (totals[0] + up_round.astype(jnp.float32), totals[1] + down_round.astype(jnp.float32)), None


def reference(tokens, grad_out, up_tiles, down_tiles, tile_rows, tile_cols, tile_count):
    hrows = HIDDEN_SIZE // TILE
    width = ROWS_DEV * TILE
    valid = jnp.arange(CAP, dtype=jnp.int32)[None, :] < tile_count[:, None]
    keep = valid.astype(up_tiles.dtype)
    grow = (tile_rows + ROWS_DEV * jnp.arange(N_TILE, dtype=jnp.int32)[:, None]).reshape(-1)
    gcol = tile_cols.reshape(-1)
    up_live = (up_tiles * keep[:, :, None, None]).reshape(N_TILE * CAP, TILE, TILE)
    down_live = (down_tiles * keep[:, :, None, None]).reshape(N_TILE * CAP, TILE, TILE)
    up_dense = jnp.zeros((COLS, TILE, hrows, TILE), up_tiles.dtype).at[gcol, :, grow, :].add(up_live).reshape(D, HIDDEN_SIZE)
    down_dense = jnp.zeros((hrows, TILE, COLS, TILE), down_tiles.dtype).at[grow, :, gcol, :].add(down_live).reshape(HIDDEN_SIZE, D)
    pre = jnp.dot(tokens, up_dense, preferred_element_type=jnp.float32)
    value, slope = gelu_pair(pre)
    hidden = value.astype(jnp.bfloat16)
    h_blocks = hidden.reshape(TOKENS, N_TILE, width).transpose(1, 0, 2)
    down_blocks = down_dense.reshape(N_TILE, width, D)
    mixed_total, _ = lax.scan(add_owner, jnp.zeros((TOKENS, D), jnp.float32), (h_blocks, down_blocks))
    mixed = mixed_total.astype(jnp.bfloat16)
    grad_hidden = jnp.dot(grad_out, down_dense.T, preferred_element_type=jnp.float32)
    grad_pre = (grad_hidden * slope).astype(jnp.bfloat16)
    d_blocks = grad_pre.reshape(TOKENS, N_TILE, width).transpose(1, 0, 2)
    up_blocks = up_dense.reshape(D, N_TILE, width).transpose(1, 2, 0)
    input_total, _ = lax.scan(add_owner, jnp.zeros((TOKENS, D), jnp.float32), (d_blocks, up_blocks))
    grad_in = input_total.astype(jnp.bfloat16)
    groups = (tokens.reshape(N_DP, TOK_DEV, D), grad_out.reshape(N_DP, TOK_DEV, D),
              hidden.reshape(N_DP, TOK_DEV, HIDDEN_SIZE), grad_pre.reshape(N_DP, TOK_DEV, HIDDEN_SIZE))
    start = (jnp.zeros((D, HIDDEN_SIZE), jnp.float32), jnp.zeros((HIDDEN_SIZE, D), jnp.float32))
    (up_sum, down_sum), _ = lax.scan(add_group, start, groups)
    up_sum = up_sum * (1.0 / N_DP)
    down_sum = down_sum * (1.0 / N_DP)
    live = valid.astype(jnp.float32)[:, :, None, None]
    grad_up = up_sum.reshape(COLS, TILE, hrows, TILE)[gcol, :, grow, :].reshape(N_TILE, CAP, TILE, TILE) * live
    grad_down = down_sum.reshape(hrows, TILE, COLS, TILE)[grow, :, gcol, :].reshape(N_TILE, CAP, TILE, TILE) * live
    return mixed, grad_in, grad_up, grad_down
```

```python
import functools

import jax
import jax.numpy as jnp
from jax import lax
from jax.experimental import pallas as pl
from jax.experimental.pallas import tpu as pltpu
from jax.sharding import PartitionSpec as P

HIDDEN_SIZE = 16384
VMEM_LIMIT = 64 * 1024 * 1024 - 65536


def gelu_pair(pre):
    curve = lax.erf(pre * 0.7071067811865476)
    value = 0.5 * pre * (1.0 + curve)
    slope = 0.5 * (1.0 + curve) + pre * jnp.exp(-0.5 * pre * pre) * 0.3989422804014327
    return (value, slope)


def dense_kernel(rows, cols, count, up, down, up_out, down_out, up_buf, down_buf, sems, out_sems):
    side = up.shape[1]
    live = count[0]

    def clear(buf):
        step = 16

        @pl.loop(0, buf.shape[0] // step)
        def _(i):
            buf[pl.ds(pl.multiple_of(i * step, step), step), :] = jnp.zeros((step, buf.shape[1]), buf.dtype)

    def up_copy(s):
        r = pl.multiple_of(rows[s] * side, side)
        c = pl.multiple_of(cols[s] * side, side)
        return pltpu.make_async_copy(up.at[s], up_buf.at[pl.ds(c, side), pl.ds(r, side)], sems.at[0])

    def down_copy(s):
        r = pl.multiple_of(rows[s] * side, side)
        c = pl.multiple_of(cols[s] * side, side)
        return pltpu.make_async_copy(down.at[s], down_buf.at[pl.ds(r, side), pl.ds(c, side)], sems.at[1])

    clear(up_buf)

    @pl.loop(0, live)
    def _(s):
        up_copy(s).start()

    clear(down_buf)

    @pl.loop(0, live)
    def _(s):
        down_copy(s).start()

    @pl.loop(0, live)
    def _(s):
        up_copy(s).wait()

    first = pltpu.make_async_copy(up_buf, up_out, out_sems.at[0])
    first.start()

    @pl.loop(0, live)
    def _(s):
        down_copy(s).wait()

    second = pltpu.make_async_copy(down_buf, down_out, out_sems.at[1])
    second.start()
    first.wait()
    second.wait()


def densify(rows, cols, count, up, down, width, hidden):
    smem = pl.BlockSpec(memory_space=pltpu.SMEM)
    hbm = pl.BlockSpec(memory_space=pl.ANY)
    return pl.pallas_call(
        dense_kernel,
        out_shape=(
            jax.ShapeDtypeStruct((width, hidden), up.dtype),
            jax.ShapeDtypeStruct((hidden, width), up.dtype),
        ),
        in_specs=[smem, smem, smem, hbm, hbm],
        out_specs=(hbm, hbm),
        scratch_shapes=[
            pltpu.VMEM((width, hidden), up.dtype),
            pltpu.VMEM((hidden, width), up.dtype),
            pltpu.SemaphoreType.DMA((2,)),
            pltpu.SemaphoreType.DMA((2,)),
        ],
        compiler_params=pltpu.CompilerParams(vmem_limit_bytes=VMEM_LIMIT),
        cost_estimate=pl.CostEstimate(flops=0, bytes_accessed=6 * width * hidden, transcendentals=0),
        name="densify",
    )(rows, cols, count, up, down)


NT = (((1,), (1,)), ((), ()))
TN = (((0,), (0,)), ((), ()))


def layer_kernel(x, up, down, hg, part, out_acc, in_acc):
    step = pl.program_id(0)
    owners, _, _, feats = x.shape

    @pl.when(step == 0)
    def _():
        out_acc[...] = jnp.zeros_like(out_acc)
        in_acc[...] = jnp.zeros_like(in_acc)

    pre = jnp.zeros(hg.shape[1:], jnp.float32)
    grad_hidden = jnp.zeros(hg.shape[1:], jnp.float32)
    for t in range(owners):
        span = slice(t * feats, (t + 1) * feats)
        pre += jnp.dot(x[t, 0], up[span, :], preferred_element_type=jnp.float32)
        grad_hidden += lax.dot_general(x[t, 1], down[:, span], NT, preferred_element_type=jnp.float32)
    value, slope = gelu_pair(pre)
    hidden = value.astype(jnp.bfloat16)
    grad_pre = (grad_hidden * slope).astype(jnp.bfloat16)
    hg[0] = hidden
    hg[1] = grad_pre
    for t in range(owners):
        span = slice(t * feats, (t + 1) * feats)
        out_acc[t] += jnp.dot(hidden, down[:, span], preferred_element_type=jnp.float32)
        in_acc[t] += lax.dot_general(grad_pre, up[span, :], NT, preferred_element_type=jnp.float32)

    @pl.when(step == pl.num_programs(0) - 1)
    def _():
        part[:, 0] = out_acc[...].astype(jnp.bfloat16)
        part[:, 1] = in_acc[...].astype(jnp.bfloat16)


def layer(x, up, down):
    owners, _, count_tok, feats = x.shape
    width, hidden = up.shape
    block = min(256, hidden)
    whole = pl.BlockSpec(x.shape, lambda h: (0, 0, 0, 0), pipeline_mode=pl.Buffered(1))
    return pl.pallas_call(
        layer_kernel,
        grid=(hidden // block,),
        out_shape=(
            jax.ShapeDtypeStruct((2, count_tok, hidden), jnp.bfloat16),
            jax.ShapeDtypeStruct(x.shape, jnp.bfloat16),
        ),
        in_specs=[
            whole,
            pl.BlockSpec((width, block), lambda h: (0, h)),
            pl.BlockSpec((block, width), lambda h: (h, 0)),
        ],
        out_specs=(
            pl.BlockSpec((2, count_tok, block), lambda h: (0, 0, h)),
            pl.BlockSpec(x.shape, lambda h: (0, 0, 0, 0)),
        ),
        scratch_shapes=[pltpu.VMEM((owners, count_tok, feats), jnp.float32)] * 2,
        compiler_params=pltpu.CompilerParams(vmem_limit_bytes=VMEM_LIMIT),
        cost_estimate=pl.CostEstimate(
            flops=8 * count_tok * width * hidden, bytes_accessed=4 * width * hidden, transcendentals=0
        ),
        name="layer",
    )(x, up, down)


def grads_kernel(scale, rows, cols, info, x, hg, grad_up, grad_down):
    group, side = grad_up.shape[0], grad_up.shape[1]
    per = x.shape[4] // side
    base = info[1] + pl.program_id(0) * group

    for j in range(group):
        s = base + j
        live = s < info[0]

        @pl.when(live)
        def _():
            r = pl.multiple_of(rows[s] * side, side)
            c = cols[s]
            owner = c // per
            f = pl.multiple_of((c - owner * per) * side, side)
            tokens = x.shape[0] * x.shape[3]
            xs = x[:, owner, 0, :, pl.ds(f, side)].reshape(tokens, side)
            dys = x[:, owner, 1, :, pl.ds(f, side)].reshape(tokens, side)
            h = hg[:, 0, :, pl.ds(r, side)].reshape(tokens, side)
            g = hg[:, 1, :, pl.ds(r, side)].reshape(tokens, side)
            grad_up[j] = lax.dot_general(xs, g, TN, preferred_element_type=jnp.float32) * scale
            grad_down[j] = lax.dot_general(h, dys, TN, preferred_element_type=jnp.float32) * scale

        @pl.when(jnp.logical_not(live))
        def _():
            grad_up[j] = jnp.zeros((side, side), jnp.float32)
            grad_down[j] = jnp.zeros((side, side), jnp.float32)


def grads(rows, cols, info, x, hg, slots, side, scale):
    smem = pl.BlockSpec(memory_space=pltpu.SMEM)
    group = min(8, slots)
    out = pl.BlockSpec((group, side, side), lambda i: (i, 0, 0))
    shape = jax.ShapeDtypeStruct((slots, side, side), jnp.float32)
    return pl.pallas_call(
        functools.partial(grads_kernel, scale),
        grid=(slots // group,),
        out_shape=(shape, shape),
        in_specs=[
            smem,
            smem,
            smem,
            pl.BlockSpec(x.shape, lambda i: (0,) * 5, pipeline_mode=pl.Buffered(1)),
            pl.BlockSpec(hg.shape, lambda i: (0,) * 4, pipeline_mode=pl.Buffered(1)),
        ],
        out_specs=(out, out),
        compiler_params=pltpu.CompilerParams(vmem_limit_bytes=VMEM_LIMIT),
        cost_estimate=pl.CostEstimate(
            flops=4 * slots * side * side * x.shape[0] * x.shape[3],
            bytes_accessed=8 * slots * side * side + 2 * x.size + 2 * hg.size,
            transcendentals=0,
        ),
        name="grads",
    )(rows, cols, info, x, hg)


def body(tokens, grad_out, up_tiles, down_tiles, tile_rows, tile_cols, tile_count):
    slots, side = up_tiles.shape[1:3]
    n_tile, n_dp = lax.axis_size("tile"), lax.axis_size("dp")
    hidden = HIDDEN_SIZE // n_tile
    width = tokens.shape[1] * n_tile
    mine = jnp.stack([tokens, grad_out])
    x = lax.all_gather(mine, "tile")
    up, down = densify(tile_rows[0], tile_cols[0], tile_count, up_tiles[0], down_tiles[0], width, hidden)
    x_all = lax.all_gather(x, "dp")
    hg, part = layer(x, up, down)
    hg_all = lax.all_gather(hg, "dp")
    total = lax.psum_scatter(part, "tile", scatter_dimension=0)
    share = slots // n_dp
    info = jnp.concatenate([tile_count, (lax.axis_index("dp") * share).astype(jnp.int32)[None]])
    grad_up, grad_down = grads(tile_rows[0], tile_cols[0], info, x_all, hg_all, share, side, 1.0 / n_dp)
    return (total[0], total[1], grad_up[None], grad_down[None])


def solution(mesh):
    placed = (
        P("dp", "tile"),
        P("dp", "tile"),
        P("tile", None, None, None),
        P("tile", None, None, None),
        P("tile", None),
        P("tile", None),
        P("tile"),
    )
    return jax.shard_map(
        body,
        mesh=mesh,
        in_specs=placed,
        out_specs=(
            P("dp", "tile"),
            P("dp", "tile"),
            P("tile", "dp", None, None),
            P("tile", "dp", None, None),
        ),
        check_vma=False,
    )
```

```python
import functools

import jax
import jax.numpy as jnp
from jax import lax
from jax.experimental import pallas as pl
from jax.experimental.pallas import tpu as pltpu
from jax.sharding import PartitionSpec as P

HIDDEN_SIZE = 16384
VMEM_LIMIT = 64 * 1024 * 1024 - 65536


def gelu_pair(pre):
    curve = lax.erf(pre * 0.7071067811865476)
    value = 0.5 * pre * (1.0 + curve)
    slope = 0.5 * (1.0 + curve) + pre * jnp.exp(-0.5 * pre * pre) * 0.3989422804014327
    return (value, slope)


def dense_kernel(rows, cols, count, up, down, up_out, down_out, up_buf, down_buf, sems, out_sems):
    side = up.shape[1]
    live = count[0]

    def clear(buf):
        step = 16

        @pl.loop(0, buf.shape[0] // step)
        def _(i):
            buf[pl.ds(pl.multiple_of(i * step, step), step), :] = jnp.zeros((step, buf.shape[1]), buf.dtype)

    def up_copy(s):
        r = pl.multiple_of(rows[s] * side, side)
        c = pl.multiple_of(cols[s] * side, side)
        return pltpu.make_async_copy(up.at[s], up_buf.at[pl.ds(c, side), pl.ds(r, side)], sems.at[0])

    def down_copy(s):
        r = pl.multiple_of(rows[s] * side, side)
        c = pl.multiple_of(cols[s] * side, side)
        return pltpu.make_async_copy(down.at[s], down_buf.at[pl.ds(r, side), pl.ds(c, side)], sems.at[1])

    clear(up_buf)

    @pl.loop(0, live)
    def _(s):
        up_copy(s).start()

    clear(down_buf)

    @pl.loop(0, live)
    def _(s):
        down_copy(s).start()

    @pl.loop(0, live)
    def _(s):
        up_copy(s).wait()

    first = pltpu.make_async_copy(up_buf, up_out, out_sems.at[0])
    first.start()

    @pl.loop(0, live)
    def _(s):
        down_copy(s).wait()

    second = pltpu.make_async_copy(down_buf, down_out, out_sems.at[1])
    second.start()
    first.wait()
    second.wait()


def densify(rows, cols, count, up, down, width, hidden):
    smem = pl.BlockSpec(memory_space=pltpu.SMEM)
    hbm = pl.BlockSpec(memory_space=pl.ANY)
    return pl.pallas_call(
        dense_kernel,
        out_shape=(
            jax.ShapeDtypeStruct((width, hidden), up.dtype),
            jax.ShapeDtypeStruct((hidden, width), up.dtype),
        ),
        in_specs=[smem, smem, smem, hbm, hbm],
        out_specs=(hbm, hbm),
        scratch_shapes=[
            pltpu.VMEM((width, hidden), up.dtype),
            pltpu.VMEM((hidden, width), up.dtype),
            pltpu.SemaphoreType.DMA((2,)),
            pltpu.SemaphoreType.DMA((2,)),
        ],
        compiler_params=pltpu.CompilerParams(vmem_limit_bytes=VMEM_LIMIT),
        cost_estimate=pl.CostEstimate(flops=0, bytes_accessed=6 * width * hidden, transcendentals=0),
        name="densify",
    )(rows, cols, count, up, down)


NT = (((1,), (1,)), ((), ()))
TN = (((0,), (0,)), ((), ()))


def layer_kernel(n_dp, n_tile, mine, up, down, x_all, hg_all, part,
                 xz, up_v, down_v, pre, hg, outbox, inbox,
                 up_sem, down_sem, own_sem, z_send, z_recv, f_send, f_recv, d_send, d_recv, e_send, e_recv,
                 h_send, h_recv, r_send, r_recv):
    n_z = n_tile // 2
    dp = lax.axis_index("dp")
    me = lax.axis_index("tile")
    z, core = me // 2, me % 2
    sib = 2 * z + (1 - core)
    feats = xz.shape[3]
    hidden = pre.shape[2]
    block = min(256, hidden)

    def to(src, dst, ssem, rsem, d, t):
        return pltpu.make_async_remote_copy(
            src_ref=src, dst_ref=dst, send_sem=ssem, recv_sem=rsem,
            device_id={"dp": d, "tile": t}, device_id_type=pl.DeviceIdType.MESH)

    def owner(j):
        return 2 * ((z + n_z - j) % n_z) + core

    def other(j):
        return 2 * ((z + n_z - j) % n_z) + 1 - core

    def up_copy(t):
        return pltpu.make_async_copy(up.at[t], up_v.at[t], up_sem.at[t])

    def down_copy(t):
        at = pl.ds(pl.multiple_of(t * feats, 128), feats)
        return pltpu.make_async_copy(down.at[:, at], down_v.at[t], down_sem.at[t])

    def z_copy(j):
        return to(xz.at[me], xz.at[me], z_send.at[j], z_recv.at[j], dp, 2 * ((z + j) % n_z) + core)

    def f_copy(j):
        return to(xz.at[owner(j)], xz.at[owner(j)], f_send.at[j], f_recv.at[j], dp, sib)

    def d_copy(k, j):
        return to(xz.at[owner(j)], x_all.at[dp, owner(j)], d_send.at[k, j], d_recv.at[k, j], (dp + k) % n_dp, me)

    def e_copy(k, j):
        slot = x_all.at[(dp + n_dp - k) % n_dp, owner(j)]
        return to(slot, slot, e_send.at[k, j], e_recv.at[k, j], dp, sib)

    def h_copy(k):
        return to(hg, hg_all.at[dp], h_send.at[k], h_recv.at[k], (dp + k) % n_dp, me)

    def r_copy(i):
        return to(outbox.at[i], inbox.at[i], r_send.at[i], r_recv.at[i], dp, (me + i) % n_tile)

    barrier = pltpu.get_barrier_semaphore()
    for i in range(1, n_tile):
        pl.semaphore_signal(barrier, inc=1, device_id={"dp": dp, "tile": (me + i) % n_tile},
                            device_id_type=pl.DeviceIdType.MESH)
    for k in range(1, n_dp):
        pl.semaphore_signal(barrier, inc=1, device_id={"dp": (dp + k) % n_dp, "tile": me},
                            device_id_type=pl.DeviceIdType.MESH)
    own = pltpu.make_async_copy(mine, xz.at[me], own_sem.at[0])
    own.start()
    for j in range(n_z):
        for t in (owner(j), other(j)):
            up_copy(t).start()
            down_copy(t).start()
    pre[...] = jnp.zeros_like(pre)
    pl.semaphore_wait(barrier, n_tile + n_dp - 2)
    own.wait()
    for j in range(1, n_z):
        z_copy(j).start()
    f_copy(0).start()
    for k in range(1, n_dp):
        d_copy(k, 0).start()

    def gather_in(t):
        up_copy(t).wait()
        down_copy(t).wait()

        @pl.loop(0, hidden // block)
        def _(b):
            at = pl.ds(pl.multiple_of(b * block, block), block)
            pre[0, :, at] += jnp.dot(xz[t, 0], up_v[t, :, at], preferred_element_type=jnp.float32)
            pre[1, :, at] += lax.dot_general(xz[t, 1], down_v[t, at, :], NT, preferred_element_type=jnp.float32)

    for j in range(n_z):
        if j:
            z_copy(j).wait_recv()
            f_copy(j).start()
            for k in range(1, n_dp):
                d_copy(k, j).start()
        gather_in(owner(j))
        f_copy(j).wait_recv()
        gather_in(other(j))

    @pl.loop(0, hidden // block)
    def _(b):
        at = pl.ds(pl.multiple_of(b * block, block), block)
        value, slope = gelu_pair(pre[0, :, at])
        hg[0, :, at] = value.astype(jnp.bfloat16)
        hg[1, :, at] = (pre[1, :, at] * slope).astype(jnp.bfloat16)

    for k in range(1, n_dp):
        h_copy(k).start()
    keep_hg = pltpu.make_async_copy(hg, hg_all.at[dp], own_sem.at[1])
    keep_hg.start()
    keep_x = pltpu.make_async_copy(xz, x_all.at[dp], own_sem.at[2])
    keep_x.start()

    def terms(i):
        t = (me + i) % n_tile
        outbox[i, 0] = jnp.dot(hg[0], down_v[t], preferred_element_type=jnp.float32).astype(jnp.bfloat16)
        outbox[i, 1] = lax.dot_general(hg[1], up_v[t], NT, preferred_element_type=jnp.float32).astype(jnp.bfloat16)

    @pl.loop(1, n_tile)
    def _(i):
        terms(i)
        r_copy(i).start()

    terms(0)
    for j in range(n_z):
        for k in range(1, n_dp):
            d_copy(k, j).wait_recv()
            e_copy(k, j).start()
    total = outbox[0].astype(jnp.float32)
    for i in range(1, n_tile):
        r_copy(i).wait_recv()
        total = total + inbox[i].astype(jnp.float32)
    part[...] = total.astype(jnp.bfloat16)
    keep_hg.wait()
    keep_x.wait()
    for j in range(n_z):
        if j:
            z_copy(j).wait_send()
        f_copy(j).wait_send()
        for k in range(1, n_dp):
            d_copy(k, j).wait_send()
            e_copy(k, j).wait()
    for k in range(1, n_dp):
        h_copy(k).wait()
    for i in range(1, n_tile):
        r_copy(i).wait_send()


def layer(mine, up, down, n_dp, n_tile):
    _, count_tok, feats = mine.shape
    width, hidden = up.shape
    n_z = n_tile // 2
    hbm = pl.BlockSpec(memory_space=pl.ANY)
    kind = jnp.bfloat16
    dma = pltpu.SemaphoreType.DMA
    box = pltpu.VMEM((n_tile, 2, count_tok, feats), kind)
    return pl.pallas_call(
        functools.partial(layer_kernel, n_dp, n_tile),
        out_shape=(
            jax.ShapeDtypeStruct((n_dp, n_tile, 2, count_tok, feats), kind),
            jax.ShapeDtypeStruct((n_dp, 2, count_tok, hidden), kind),
            jax.ShapeDtypeStruct(mine.shape, kind),
        ),
        in_specs=[hbm, hbm, hbm],
        out_specs=(hbm, hbm, pl.BlockSpec(memory_space=pltpu.VMEM)),
        scratch_shapes=[
            box,
            pltpu.VMEM((n_tile, feats, hidden), kind),
            pltpu.VMEM((n_tile, hidden, feats), kind),
            pltpu.VMEM((2, count_tok, hidden), jnp.float32),
            pltpu.VMEM((2, count_tok, hidden), kind),
            box,
            box,
            dma((n_tile,)),
            dma((n_tile,)),
            dma((3,)),
            dma((n_z,)),
            dma((n_z,)),
            dma((n_z,)),
            dma((n_z,)),
            dma((n_dp, n_z)),
            dma((n_dp, n_z)),
            dma((n_dp, n_z)),
            dma((n_dp, n_z)),
            dma((n_dp,)),
            dma((n_dp,)),
            dma((n_tile,)),
            dma((n_tile,)),
        ],
        compiler_params=pltpu.CompilerParams(
            vmem_limit_bytes=VMEM_LIMIT, collective_id=0, has_side_effects=True
        ),
        name="layer",
    )(mine, up.reshape(n_tile, feats, hidden), down)


def grads_kernel(scale, rows, cols, info, x, hg, grad_up, grad_down):
    group, side = grad_up.shape[0], grad_up.shape[1]
    per = x.shape[4] // side
    base = info[1] + pl.program_id(0) * group

    for j in range(group):
        s = base + j
        live = s < info[0]

        @pl.when(live)
        def _():
            r = pl.multiple_of(rows[s] * side, side)
            c = cols[s]
            owner = c // per
            f = pl.multiple_of((c - owner * per) * side, side)
            tokens = x.shape[0] * x.shape[3]
            xs = x[:, owner, 0, :, pl.ds(f, side)].reshape(tokens, side)
            dys = x[:, owner, 1, :, pl.ds(f, side)].reshape(tokens, side)
            h = hg[:, 0, :, pl.ds(r, side)].reshape(tokens, side)
            g = hg[:, 1, :, pl.ds(r, side)].reshape(tokens, side)
            grad_up[j] = lax.dot_general(xs, g, TN, preferred_element_type=jnp.float32) * scale
            grad_down[j] = lax.dot_general(h, dys, TN, preferred_element_type=jnp.float32) * scale

        @pl.when(jnp.logical_not(live))
        def _():
            grad_up[j] = jnp.zeros((side, side), jnp.float32)
            grad_down[j] = jnp.zeros((side, side), jnp.float32)


def grads(rows, cols, info, x, hg, slots, side, scale):
    smem = pl.BlockSpec(memory_space=pltpu.SMEM)
    group = min(8, slots)
    out = pl.BlockSpec((group, side, side), lambda i: (i, 0, 0))
    shape = jax.ShapeDtypeStruct((slots, side, side), jnp.float32)
    return pl.pallas_call(
        functools.partial(grads_kernel, scale),
        grid=(slots // group,),
        out_shape=(shape, shape),
        in_specs=[
            smem,
            smem,
            smem,
            pl.BlockSpec(x.shape, lambda i: (0,) * 5, pipeline_mode=pl.Buffered(1)),
            pl.BlockSpec(hg.shape, lambda i: (0,) * 4, pipeline_mode=pl.Buffered(1)),
        ],
        out_specs=(out, out),
        compiler_params=pltpu.CompilerParams(vmem_limit_bytes=VMEM_LIMIT),
        cost_estimate=pl.CostEstimate(
            flops=4 * slots * side * side * x.shape[0] * x.shape[3],
            bytes_accessed=8 * slots * side * side + 2 * x.size + 2 * hg.size,
            transcendentals=0,
        ),
        name="grads",
    )(rows, cols, info, x, hg)


def body(tokens, grad_out, up_tiles, down_tiles, tile_rows, tile_cols, tile_count):
    slots, side = up_tiles.shape[1:3]
    n_tile, n_dp = lax.axis_size("tile"), lax.axis_size("dp")
    hidden = HIDDEN_SIZE // n_tile
    width = tokens.shape[1] * n_tile
    mine = jnp.stack([tokens, grad_out])
    up, down = densify(tile_rows[0], tile_cols[0], tile_count, up_tiles[0], down_tiles[0], width, hidden)
    x_all, hg_all, total = layer(mine, up, down, n_dp, n_tile)
    share = slots // n_dp
    info = jnp.concatenate([tile_count, (lax.axis_index("dp") * share).astype(jnp.int32)[None]])
    grad_up, grad_down = grads(tile_rows[0], tile_cols[0], info, x_all, hg_all, share, side, 1.0 / n_dp)
    return (total[0], total[1], grad_up[None], grad_down[None])


def solution(mesh):
    placed = (
        P("dp", "tile"),
        P("dp", "tile"),
        P("tile", None, None, None),
        P("tile", None, None, None),
        P("tile", None),
        P("tile", None),
        P("tile"),
    )
    return jax.shard_map(
        body,
        mesh=mesh,
        in_specs=placed,
        out_specs=(
            P("dp", "tile"),
            P("dp", "tile"),
            P("tile", "dp", None, None),
            P("tile", "dp", None, None),
        ),
        check_vma=False,
    )
```

```python
import functools

import jax
import jax.numpy as jnp
from jax import lax
from jax.experimental import pallas as pl
from jax.experimental.pallas import tpu as pltpu
from jax.sharding import PartitionSpec as P

HIDDEN_SIZE = 16384
VMEM_LIMIT = 64 * 1024 * 1024 - 65536


def gelu_pair(pre):
    curve = lax.erf(pre * 0.7071067811865476)
    value = 0.5 * pre * (1.0 + curve)
    slope = 0.5 * (1.0 + curve) + pre * jnp.exp(-0.5 * pre * pre) * 0.3989422804014327
    return (value, slope)


NT = (((1,), (1,)), ((), ()))
TN = (((0,), (0,)), ((), ()))


def layer_kernel(n_dp, n_tile, slot_of, tokens, grad_out, up, down, x_all, hg_all, mixed, grad_in,
                 xz, up_t, down_t, up_v, down_v, pre, hg, outbox, inbox,
                 own_sem, z_send, z_recv, f_send, f_recv, d_send, d_recv, l_send, l_recv, e_send, e_recv,
                 h_send, h_recv, m_send, m_recv, r_send, r_recv):
    n_z = n_tile // 2
    dp = lax.axis_index("dp")
    me = lax.axis_index("tile")
    z, core = me // 2, me % 2
    sib = 2 * z + (1 - core)
    feats = xz.shape[3]
    hidden = pre.shape[2]
    slots, side = up.shape[0], up.shape[1]
    block = min(256, hidden)
    pieces = hg.shape[0]
    piece = hg.shape[3]
    square = n_dp == 4
    if square:
        x_next = 2 * (dp // 2) + 1 - dp % 2
        y_next = 2 * (1 - dp // 2) + dp % 2
        across = n_dp - 1 - dp
        targets = sources = [x_next, y_next]
        arrivals = [x_next, y_next, across]
    else:
        targets = [(dp + k) % n_dp for k in range(1, n_dp)]
        sources = arrivals = [(dp + n_dp - k) % n_dp for k in range(1, n_dp)]
    direct = range(len(targets))

    def to(src, dst, ssem, rsem, d, t):
        return pltpu.make_async_remote_copy(
            src_ref=src, dst_ref=dst, send_sem=ssem, recv_sem=rsem,
            device_id={"dp": d, "tile": t}, device_id_type=pl.DeviceIdType.MESH)

    def owner(j):
        return 2 * ((z + n_z - j) % n_z) + core

    def other(j):
        return 2 * ((z + n_z - j) % n_z) + 1 - core

    def z_copy(j):
        return to(xz.at[me], xz.at[me], z_send.at[j], z_recv.at[j], dp, 2 * ((z + j) % n_z) + core)

    def f_copy(j):
        return to(xz.at[owner(j)], xz.at[owner(j)], f_send.at[j], f_recv.at[j], dp, sib)

    def d_copy(k, j):
        return to(xz.at[owner(j)], x_all.at[dp, owner(j)], d_send.at[k, j], d_recv.at[k, j], targets[k], me)

    def l_copy(k, j):
        slot = x_all.at[sources[k], owner(j), k]
        return to(slot, slot, l_send.at[k, j], l_recv.at[k, j], targets[1 - k], me)

    def e_copy(k, j):
        slot = x_all.at[arrivals[k], owner(j)]
        return to(slot, slot, e_send.at[k, j], e_recv.at[k, j], dp, sib)

    def h_copy(k, p):
        return to(hg.at[p], hg_all.at[dp, p], h_send.at[k, p], h_recv.at[k, p], targets[k], me)

    def m_copy(k, p):
        slot = hg_all.at[sources[k], p, k]
        return to(slot, slot, m_send.at[k, p], m_recv.at[k, p], targets[1 - k], me)

    def r_copy(i):
        return to(outbox.at[i], inbox.at[i], r_send.at[i], r_recv.at[i], dp, (me + i) % n_tile)

    def landed(j):
        for k in direct:
            d_copy(k, j).wait_recv()
            if square:
                l_copy(k, j).start()
            e_copy(k, j).start()

    barrier = pltpu.get_barrier_semaphore()
    for i in range(1, n_tile):
        pl.semaphore_signal(barrier, inc=1, device_id={"dp": dp, "tile": (me + i) % n_tile},
                            device_id_type=pl.DeviceIdType.MESH)
    for k in direct:
        pl.semaphore_signal(barrier, inc=1, device_id={"dp": targets[k], "tile": me},
                            device_id_type=pl.DeviceIdType.MESH)
    own = [pltpu.make_async_copy(tokens, xz.at[me, 0], own_sem.at[0]),
           pltpu.make_async_copy(grad_out, xz.at[me, 1], own_sem.at[1])]
    load = [pltpu.make_async_copy(up, up_t.at[pl.ds(0, slots)], own_sem.at[2]),
            pltpu.make_async_copy(down, down_t.at[pl.ds(0, slots)], own_sem.at[3])]
    for copy in own + load:
        copy.start()
    up_t[slots] = jnp.zeros((side, side), up_t.dtype)
    down_t[slots] = jnp.zeros((side, side), down_t.dtype)
    pre[...] = jnp.zeros_like(pre)
    pl.semaphore_wait(barrier, n_tile - 1 + len(targets))
    for copy in own:
        copy.wait()
    for j in range(1, n_z):
        z_copy(j).start()
    f_copy(0).start()
    for k in direct:
        d_copy(k, 0).start()
    for copy in load:
        copy.wait()

    def gather_in(t):
        wide = feats // side
        high = hidden // side

        @pl.loop(0, high)
        def _(r):
            at = pl.ds(pl.multiple_of(r * side, side), side)
            for c in range(wide):
                slot = slot_of[(t * wide + c) * high + r]
                up_v[t, c * side:(c + 1) * side, at] = up_t[slot]
                down_v[t, at, c * side:(c + 1) * side] = down_t[slot]

        @pl.loop(0, hidden // block)
        def _(b):
            at = pl.ds(pl.multiple_of(b * block, block), block)
            pre[0, :, at] += jnp.dot(xz[t, 0], up_v[t, :, at], preferred_element_type=jnp.float32)
            pre[1, :, at] += lax.dot_general(xz[t, 1], down_v[t, at, :], NT, preferred_element_type=jnp.float32)

    for j in range(n_z):
        if j:
            z_copy(j).wait_recv()
            f_copy(j).start()
            for k in direct:
                d_copy(k, j).start()
        gather_in(owner(j))
        f_copy(j).wait_recv()
        gather_in(other(j))
        if j:
            landed(j - 1)

    for p in range(pieces):
        value, slope = gelu_pair(pre[0, :, p * piece:(p + 1) * piece])
        hg[p, 0] = value.astype(jnp.bfloat16)
        hg[p, 1] = (pre[1, :, p * piece:(p + 1) * piece] * slope).astype(jnp.bfloat16)
        for k in direct:
            h_copy(k, p).start()
    keep = [pltpu.make_async_copy(hg, hg_all.at[dp], own_sem.at[0]),
            pltpu.make_async_copy(xz, x_all.at[dp], own_sem.at[1])]
    for copy in keep:
        copy.start()

    def terms(i):
        t = (me + i) % n_tile
        out = jnp.zeros((pre.shape[1], feats), jnp.float32)
        back = jnp.zeros((pre.shape[1], feats), jnp.float32)
        for p in range(pieces):
            span = slice(p * piece, (p + 1) * piece)
            out += jnp.dot(hg[p, 0], down_v[t, span, :], preferred_element_type=jnp.float32)
            back += lax.dot_general(hg[p, 1], up_v[t, :, span], NT, preferred_element_type=jnp.float32)
        outbox[i, 0] = out.astype(jnp.bfloat16)
        outbox[i, 1] = back.astype(jnp.bfloat16)

    @pl.loop(1, n_tile)
    def _(i):
        terms(i)
        r_copy(i).start()

    landed(n_z - 1)
    terms(0)
    for p in range(pieces):
        if square:
            for k in direct:
                h_copy(k, p).wait_recv()
                m_copy(k, p).start()
    if square:
        for j in range(n_z):
            for k in direct:
                l_copy(k, j).wait_recv()
            e_copy(2, j).start()
    mix = outbox[0, 0].astype(jnp.float32)
    back = outbox[0, 1].astype(jnp.float32)
    for i in range(1, n_tile):
        r_copy(i).wait_recv()
        mix = mix + inbox[i, 0].astype(jnp.float32)
        back = back + inbox[i, 1].astype(jnp.float32)
    mixed[...] = mix.astype(jnp.bfloat16)
    grad_in[...] = back.astype(jnp.bfloat16)
    for copy in keep:
        copy.wait()
    for j in range(n_z):
        if j:
            z_copy(j).wait_send()
        f_copy(j).wait_send()
        for k in direct:
            d_copy(k, j).wait_send()
            if square:
                l_copy(k, j).wait_send()
        for k in range(n_dp - 1):
            e_copy(k, j).wait()
    for p in range(pieces):
        for k in direct:
            h_copy(k, p).wait_send()
            if square:
                m_copy(k, p).wait()
            else:
                h_copy(k, p).wait_recv()
    for i in range(1, n_tile):
        r_copy(i).wait_send()


def layer(slot_of, tokens, grad_out, up, down, n_dp, n_tile):
    count_tok, feats = tokens.shape
    slots, side = up.shape[:2]
    hidden = HIDDEN_SIZE // n_tile
    n_z = n_tile // 2
    pieces = min(4, hidden // side)
    hbm = pl.BlockSpec(memory_space=pl.ANY)
    vmem = pl.BlockSpec(memory_space=pltpu.VMEM)
    kind = jnp.bfloat16
    dma = pltpu.SemaphoreType.DMA
    box = pltpu.VMEM((n_tile, 2, count_tok, feats), kind)
    packed = (pieces, 2, count_tok, hidden // pieces)
    pairs = [dma((n_dp, n_z)), dma((n_dp, n_z))]
    sends = [dma((n_dp, pieces)), dma((n_dp, pieces))]
    return pl.pallas_call(
        functools.partial(layer_kernel, n_dp, n_tile),
        out_shape=(
            jax.ShapeDtypeStruct((n_dp, n_tile, 2, count_tok, feats), kind),
            jax.ShapeDtypeStruct((n_dp,) + packed, kind),
            jax.ShapeDtypeStruct(tokens.shape, kind),
            jax.ShapeDtypeStruct(tokens.shape, kind),
        ),
        in_specs=[pl.BlockSpec(memory_space=pltpu.SMEM), hbm, hbm, hbm, hbm],
        out_specs=(hbm, hbm, vmem, vmem),
        scratch_shapes=[
            box,
            pltpu.VMEM((slots + 1, side, side), kind),
            pltpu.VMEM((slots + 1, side, side), kind),
            pltpu.VMEM((n_tile, feats, hidden), kind),
            pltpu.VMEM((n_tile, hidden, feats), kind),
            pltpu.VMEM((2, count_tok, hidden), jnp.float32),
            pltpu.VMEM(packed, kind),
            box,
            box,
            dma((4,)),
            dma((n_z,)),
            dma((n_z,)),
            dma((n_z,)),
            dma((n_z,)),
        ] + pairs * 3 + sends * 2 + [
            dma((n_tile,)),
            dma((n_tile,)),
        ],
        compiler_params=pltpu.CompilerParams(
            vmem_limit_bytes=VMEM_LIMIT, collective_id=0, has_side_effects=True
        ),
        name="layer",
    )(slot_of, tokens, grad_out, up, down)


def grads_kernel(scale, rows, cols, info, x, hg, grad_up, grad_down):
    group, side = grad_up.shape[0], grad_up.shape[1]
    per = x.shape[4] // side
    wide = hg.shape[4] // side
    base = info[1] + pl.program_id(0) * group

    for j in range(group):
        s = base + j
        live = s < info[0]

        @pl.when(live)
        def _():
            c = cols[s]
            owner = c // per
            f = pl.multiple_of((c - owner * per) * side, side)
            tokens = x.shape[0] * x.shape[3]
            xs = x[:, owner, 0, :, pl.ds(f, side)].reshape(tokens, side)
            dys = x[:, owner, 1, :, pl.ds(f, side)].reshape(tokens, side)
            p = rows[s] // wide
            r = pl.multiple_of((rows[s] - p * wide) * side, side)
            h = hg[:, p, 0, :, pl.ds(r, side)].reshape(tokens, side)
            g = hg[:, p, 1, :, pl.ds(r, side)].reshape(tokens, side)
            grad_up[j] = lax.dot_general(xs, g, TN, preferred_element_type=jnp.float32) * scale
            grad_down[j] = lax.dot_general(h, dys, TN, preferred_element_type=jnp.float32) * scale

        @pl.when(jnp.logical_not(live))
        def _():
            grad_up[j] = jnp.zeros((side, side), jnp.float32)
            grad_down[j] = jnp.zeros((side, side), jnp.float32)


def grads(rows, cols, info, x, hg, slots, side, scale):
    smem = pl.BlockSpec(memory_space=pltpu.SMEM)
    group = min(8, slots)
    out = pl.BlockSpec((group, side, side), lambda i: (i, 0, 0))
    shape = jax.ShapeDtypeStruct((slots, side, side), jnp.float32)
    return pl.pallas_call(
        functools.partial(grads_kernel, scale),
        grid=(slots // group,),
        out_shape=(shape, shape),
        in_specs=[
            smem,
            smem,
            smem,
            pl.BlockSpec(x.shape, lambda i: (0,) * 5, pipeline_mode=pl.Buffered(1)),
            pl.BlockSpec(hg.shape, lambda i: (0,) * 5, pipeline_mode=pl.Buffered(1)),
        ],
        out_specs=(out, out),
        compiler_params=pltpu.CompilerParams(vmem_limit_bytes=VMEM_LIMIT),
        cost_estimate=pl.CostEstimate(
            flops=4 * slots * side * side * x.shape[0] * x.shape[3],
            bytes_accessed=8 * slots * side * side + 2 * x.size + 2 * hg.size,
            transcendentals=0,
        ),
        name="grads",
    )(rows, cols, info, x, hg)


def body(tokens, grad_out, up_tiles, down_tiles, tile_rows, tile_cols, tile_count):
    slots, side = up_tiles.shape[1:3]
    n_tile, n_dp = lax.axis_size("tile"), lax.axis_size("dp")
    high = HIDDEN_SIZE // (n_tile * side)
    cells = high * (tokens.shape[1] * n_tile // side)
    number = jnp.arange(slots, dtype=jnp.int32)
    place = jnp.where(number < tile_count[0], tile_cols[0] * high + tile_rows[0], -1)
    hit = place[None, :] == jnp.arange(cells, dtype=jnp.int32)[:, None]
    slot_of = jnp.min(jnp.where(hit, number[None, :], slots), axis=1)
    x_all, hg_all, mixed, grad_in = layer(
        slot_of, tokens, grad_out, up_tiles[0], down_tiles[0], n_dp, n_tile
    )
    share = slots // n_dp
    info = jnp.concatenate([tile_count, (lax.axis_index("dp") * share).astype(jnp.int32)[None]])
    grad_up, grad_down = grads(tile_rows[0], tile_cols[0], info, x_all, hg_all, share, side, 1.0 / n_dp)
    return (mixed, grad_in, grad_up[None], grad_down[None])


def solution(mesh):
    placed = (
        P("dp", "tile"),
        P("dp", "tile"),
        P("tile", None, None, None),
        P("tile", None, None, None),
        P("tile", None),
        P("tile", None),
        P("tile"),
    )
    return jax.shard_map(
        body,
        mesh=mesh,
        in_specs=placed,
        out_specs=(
            P("dp", "tile"),
            P("dp", "tile"),
            P("tile", "dp", None, None),
            P("tile", "dp", None, None),
        ),
        check_vma=False,
    )
```

```python
import functools

import jax
import jax.numpy as jnp
from jax import lax
from jax.experimental import pallas as pl
from jax.experimental.pallas import tpu as pltpu
from jax.sharding import PartitionSpec as P

HIDDEN_SIZE = 16384
VMEM_LIMIT = 64 * 1024 * 1024 - 65536


def gelu_pair(pre):
    curve = lax.erf(pre * 0.7071067811865476)
    value = 0.5 * pre * (1.0 + curve)
    slope = 0.5 * (1.0 + curve) + pre * jnp.exp(-0.5 * pre * pre) * 0.3989422804014327
    return (value, slope)


NT = (((1,), (1,)), ((), ()))
TN = (((0,), (0,)), ((), ()))


def layer_kernel(n_dp, n_tile, slot_of, tokens, grad_out, up, down, x_all, hg_all, part,
                 xz, up_t, down_t, up_v, down_v, pre, hg, outbox, inbox,
                 own_sem, z_send, z_recv, f_send, f_recv, d_send, d_recv, l_send, l_recv, e_send, e_recv,
                 h_send, h_recv, m_send, m_recv, r_send, r_recv):
    n_z = n_tile // 2
    dp = lax.axis_index("dp")
    me = lax.axis_index("tile")
    z, core = me // 2, me % 2
    sib = 2 * z + (1 - core)
    feats = xz.shape[3]
    hidden = pre.shape[2]
    slots, side = up.shape[0], up.shape[1]
    block = min(256, hidden)
    pieces = hg.shape[0]
    piece = hg.shape[3]
    square = n_dp == 4
    if square:
        x_next = 2 * (dp // 2) + 1 - dp % 2
        y_next = 2 * (1 - dp // 2) + dp % 2
        across = n_dp - 1 - dp
        targets = sources = [x_next, y_next]
        arrivals = [x_next, y_next, across]
    else:
        targets = [(dp + k) % n_dp for k in range(1, n_dp)]
        sources = arrivals = [(dp + n_dp - k) % n_dp for k in range(1, n_dp)]
    direct = range(len(targets))

    def to(src, dst, ssem, rsem, d, t):
        return pltpu.make_async_remote_copy(
            src_ref=src, dst_ref=dst, send_sem=ssem, recv_sem=rsem,
            device_id={"dp": d, "tile": t}, device_id_type=pl.DeviceIdType.MESH)

    def owner(j):
        return 2 * ((z + n_z - j) % n_z) + core

    def other(j):
        return 2 * ((z + n_z - j) % n_z) + 1 - core

    def z_copy(j):
        return to(xz.at[me], xz.at[me], z_send.at[j], z_recv.at[j], dp, 2 * ((z + j) % n_z) + core)

    def f_copy(j):
        return to(xz.at[owner(j)], xz.at[owner(j)], f_send.at[j], f_recv.at[j], dp, sib)

    def d_copy(k, j):
        return to(xz.at[owner(j)], x_all.at[dp, owner(j)], d_send.at[k, j], d_recv.at[k, j], targets[k], me)

    def l_copy(k, j):
        slot = x_all.at[sources[k], owner(j), k]
        return to(slot, slot, l_send.at[k, j], l_recv.at[k, j], targets[1 - k], me)

    def e_copy(k, j):
        slot = x_all.at[arrivals[k], owner(j)]
        return to(slot, slot, e_send.at[k, j], e_recv.at[k, j], dp, sib)

    def h_copy(k, p):
        return to(hg.at[p], hg_all.at[dp, p], h_send.at[k, p], h_recv.at[k, p], targets[k], me)

    def m_copy(k, p):
        slot = hg_all.at[sources[k], p, k]
        return to(slot, slot, m_send.at[k, p], m_recv.at[k, p], targets[1 - k], me)

    def s_copy(j):
        return to(outbox.at[j], inbox.at[j], r_send.at[j], r_recv.at[j], dp, sib)

    def r_copy(j):
        i = n_z + j
        return to(outbox.at[i], inbox.at[i], r_send.at[i], r_recv.at[i], dp, 2 * ((z + j) % n_z) + core)

    def landed(j):
        for k in direct:
            d_copy(k, j).wait_recv()
            if square:
                l_copy(k, j).start()
            e_copy(k, j).start()

    barrier = pltpu.get_barrier_semaphore()
    for t in [sib] + [2 * ((z + j) % n_z) + core for j in range(1, n_z)]:
        pl.semaphore_signal(barrier, inc=1, device_id={"dp": dp, "tile": t},
                            device_id_type=pl.DeviceIdType.MESH)
    for k in direct:
        pl.semaphore_signal(barrier, inc=1, device_id={"dp": targets[k], "tile": me},
                            device_id_type=pl.DeviceIdType.MESH)
    own = [pltpu.make_async_copy(tokens, xz.at[me, 0], own_sem.at[0]),
           pltpu.make_async_copy(grad_out, xz.at[me, 1], own_sem.at[1])]
    load = [pltpu.make_async_copy(up, up_t.at[pl.ds(0, slots)], own_sem.at[2]),
            pltpu.make_async_copy(down, down_t.at[pl.ds(0, slots)], own_sem.at[3])]
    for copy in own + load:
        copy.start()
    up_t[slots] = jnp.zeros((side, side), up_t.dtype)
    down_t[slots] = jnp.zeros((side, side), down_t.dtype)
    pre[...] = jnp.zeros_like(pre)
    pl.semaphore_wait(barrier, n_z + len(targets))
    for copy in own:
        copy.wait()
    for j in range(1, n_z):
        z_copy(j).start()
    f_copy(0).start()
    for k in direct:
        d_copy(k, 0).start()
    for copy in load:
        copy.wait()

    def gather_in(t):
        wide = feats // side
        high = hidden // side

        @pl.loop(0, high)
        def _(r):
            at = pl.ds(pl.multiple_of(r * side, side), side)
            for c in range(wide):
                slot = slot_of[(t * wide + c) * high + r]
                up_v[t, c * side:(c + 1) * side, at] = up_t[slot]
                down_v[t, at, c * side:(c + 1) * side] = down_t[slot]

        @pl.loop(0, hidden // block)
        def _(b):
            at = pl.ds(pl.multiple_of(b * block, block), block)
            pre[0, :, at] += jnp.dot(xz[t, 0], up_v[t, :, at], preferred_element_type=jnp.float32)
            pre[1, :, at] += lax.dot_general(xz[t, 1], down_v[t, at, :], NT, preferred_element_type=jnp.float32)

    for j in range(n_z):
        if j:
            z_copy(j).wait_recv()
            f_copy(j).start()
            for k in direct:
                d_copy(k, j).start()
        gather_in(owner(j))
        f_copy(j).wait_recv()
        gather_in(other(j))
        if j:
            landed(j - 1)

    for p in range(pieces):
        value, slope = gelu_pair(pre[0, :, p * piece:(p + 1) * piece])
        hg[p, 0] = value.astype(jnp.bfloat16)
        hg[p, 1] = (pre[1, :, p * piece:(p + 1) * piece] * slope).astype(jnp.bfloat16)
        for k in direct:
            h_copy(k, p).start()
    keep = [pltpu.make_async_copy(hg, hg_all.at[dp], own_sem.at[0]),
            pltpu.make_async_copy(xz, x_all.at[dp], own_sem.at[1])]
    for copy in keep:
        copy.start()

    def terms(t):
        out = jnp.zeros((pre.shape[1], feats), jnp.float32)
        back = jnp.zeros((pre.shape[1], feats), jnp.float32)
        for p in range(pieces):
            span = slice(p * piece, (p + 1) * piece)
            out += jnp.dot(hg[p, 0], down_v[t, span, :], preferred_element_type=jnp.float32)
            back += lax.dot_general(hg[p, 1], up_v[t, :, span], NT, preferred_element_type=jnp.float32)
        return out, back

    @pl.loop(0, n_z)
    def _(j):
        out, back = terms(2 * ((z + j) % n_z) + 1 - core)
        outbox[j, 0] = out.astype(jnp.bfloat16)
        outbox[j, 1] = back.astype(jnp.bfloat16)
        s_copy(j).start()

    def merged(j):
        out, back = terms(2 * ((z + j) % n_z) + core)
        s_copy(j).wait_recv()
        outbox[n_z + j, 0] = (out + inbox[j, 0].astype(jnp.float32)).astype(jnp.bfloat16)
        outbox[n_z + j, 1] = (back + inbox[j, 1].astype(jnp.float32)).astype(jnp.bfloat16)

    @pl.loop(1, n_z)
    def _(j):
        merged(j)
        r_copy(j).start()

    landed(n_z - 1)
    merged(0)
    for p in range(pieces):
        if square:
            for k in direct:
                h_copy(k, p).wait_recv()
                m_copy(k, p).start()
    if square:
        for j in range(n_z):
            for k in direct:
                l_copy(k, j).wait_recv()
            e_copy(2, j).start()
    for half in range(2):
        total = outbox[n_z, half].astype(jnp.float32)
        for j in range(1, n_z):
            if half == 0:
                r_copy(j).wait_recv()
            total = total + inbox[n_z + j, half].astype(jnp.float32)
        part[half] = total.astype(jnp.bfloat16)
    for copy in keep:
        copy.wait()
    for j in range(n_z):
        if j:
            z_copy(j).wait_send()
        f_copy(j).wait_send()
        for k in direct:
            d_copy(k, j).wait_send()
            if square:
                l_copy(k, j).wait_send()
        for k in range(n_dp - 1):
            e_copy(k, j).wait()
    for p in range(pieces):
        for k in direct:
            h_copy(k, p).wait_send()
            if square:
                m_copy(k, p).wait()
            else:
                h_copy(k, p).wait_recv()
    for j in range(n_z):
        s_copy(j).wait_send()
        if j:
            r_copy(j).wait_send()


def layer(slot_of, tokens, grad_out, up, down, n_dp, n_tile):
    count_tok, feats = tokens.shape
    slots, side = up.shape[:2]
    hidden = HIDDEN_SIZE // n_tile
    n_z = n_tile // 2
    pieces = min(4, hidden // side)
    hbm = pl.BlockSpec(memory_space=pl.ANY)
    vmem = pl.BlockSpec(memory_space=pltpu.VMEM)
    kind = jnp.bfloat16
    dma = pltpu.SemaphoreType.DMA
    box = pltpu.VMEM((n_tile, 2, count_tok, feats), kind)
    packed = (pieces, 2, count_tok, hidden // pieces)
    pairs = [dma((n_dp, n_z)), dma((n_dp, n_z))]
    sends = [dma((n_dp, pieces)), dma((n_dp, pieces))]
    return pl.pallas_call(
        functools.partial(layer_kernel, n_dp, n_tile),
        out_shape=(
            jax.ShapeDtypeStruct((n_dp, n_tile, 2, count_tok, feats), kind),
            jax.ShapeDtypeStruct((n_dp,) + packed, kind),
            jax.ShapeDtypeStruct((2,) + tokens.shape, kind),
        ),
        in_specs=[pl.BlockSpec(memory_space=pltpu.SMEM), hbm, hbm, hbm, hbm],
        out_specs=(hbm, hbm, vmem),
        scratch_shapes=[
            box,
            pltpu.VMEM((slots + 1, side, side), kind),
            pltpu.VMEM((slots + 1, side, side), kind),
            pltpu.VMEM((n_tile, feats, hidden), kind),
            pltpu.VMEM((n_tile, hidden, feats), kind),
            pltpu.VMEM((2, count_tok, hidden), jnp.float32),
            pltpu.VMEM(packed, kind),
            box,
            box,
            dma((4,)),
            dma((n_z,)),
            dma((n_z,)),
            dma((n_z,)),
            dma((n_z,)),
        ] + pairs * 3 + sends * 2 + [
            dma((n_tile,)),
            dma((n_tile,)),
        ],
        compiler_params=pltpu.CompilerParams(
            vmem_limit_bytes=VMEM_LIMIT, collective_id=0, has_side_effects=True
        ),
        name="layer",
    )(slot_of, tokens, grad_out, up, down)


def grads_kernel(scale, rows, cols, info, x, hg, part, grad_up, grad_down, mixed, grad_in):
    group, side = grad_up.shape[0], grad_up.shape[1]
    per = x.shape[4] // side
    wide = hg.shape[4] // side
    base = info[1] + pl.program_id(0) * group
    tokens = x.shape[0] * x.shape[3]

    @pl.when(pl.program_id(0) == 0)
    def _():
        mixed[...] = part[0]
        grad_in[...] = part[1]

    @pl.when(base < info[0])
    def _():
        for j in range(group):
            s = base + j
            owner = cols[s] // per
            f = pl.multiple_of((cols[s] - owner * per) * side, side)
            p = rows[s] // wide
            r = pl.multiple_of((rows[s] - p * wide) * side, side)
            xs = x[:, owner, 0, :, pl.ds(f, side)].reshape(tokens, side)
            dys = x[:, owner, 1, :, pl.ds(f, side)].reshape(tokens, side)
            h = hg[:, p, 0, :, pl.ds(r, side)].reshape(tokens, side)
            g = hg[:, p, 1, :, pl.ds(r, side)].reshape(tokens, side)
            up_sum = lax.dot_general(xs, g, TN, preferred_element_type=jnp.float32) * scale
            down_sum = lax.dot_general(h, dys, TN, preferred_element_type=jnp.float32) * scale
            grad_up[j] = jnp.where(s < info[0], up_sum, 0.0)
            grad_down[j] = jnp.where(s < info[0], down_sum, 0.0)

    @pl.when(base >= info[0])
    def _():
        grad_up[...] = jnp.zeros_like(grad_up)
        grad_down[...] = jnp.zeros_like(grad_down)


def grads(rows, cols, info, x, hg, part, slots, side, scale):
    smem = pl.BlockSpec(memory_space=pltpu.SMEM)
    group = min(8, slots)
    out = pl.BlockSpec((group, side, side), lambda i: (i, 0, 0))
    shape = jax.ShapeDtypeStruct((slots, side, side), jnp.float32)
    flat = jax.ShapeDtypeStruct(part.shape[1:], part.dtype)
    flat_spec = pl.BlockSpec(part.shape[1:], lambda i: (0, 0))
    return pl.pallas_call(
        functools.partial(grads_kernel, scale),
        grid=(slots // group,),
        out_shape=(shape, shape, flat, flat),
        in_specs=[
            smem,
            smem,
            smem,
            pl.BlockSpec(x.shape, lambda i: (0,) * 5, pipeline_mode=pl.Buffered(1)),
            pl.BlockSpec(hg.shape, lambda i: (0,) * 5, pipeline_mode=pl.Buffered(1)),
            pl.BlockSpec(part.shape, lambda i: (0,) * 3, pipeline_mode=pl.Buffered(1)),
        ],
        out_specs=(out, out, flat_spec, flat_spec),
        compiler_params=pltpu.CompilerParams(vmem_limit_bytes=VMEM_LIMIT),
        name="grads",
    )(rows, cols, info, x, hg, part)


def body(tokens, grad_out, up_tiles, down_tiles, tile_rows, tile_cols, tile_count):
    slots, side = up_tiles.shape[1:3]
    n_tile, n_dp = lax.axis_size("tile"), lax.axis_size("dp")
    high = HIDDEN_SIZE // (n_tile * side)
    cells = high * (tokens.shape[1] * n_tile // side)
    number = jnp.arange(slots, dtype=jnp.int32)
    place = jnp.where(number < tile_count[0], tile_cols[0] * high + tile_rows[0], -1)
    hit = place[None, :] == jnp.arange(cells, dtype=jnp.int32)[:, None]
    slot_of = jnp.min(jnp.where(hit, number[None, :], slots), axis=1)
    x_all, hg_all, part = layer(
        slot_of, tokens, grad_out, up_tiles[0], down_tiles[0], n_dp, n_tile
    )
    share = slots // n_dp
    info = jnp.concatenate([tile_count, (lax.axis_index("dp") * share).astype(jnp.int32)[None]])
    grad_up, grad_down, mixed, grad_in = grads(
        tile_rows[0], tile_cols[0], info, x_all, hg_all, part, share, side, 1.0 / n_dp
    )
    return (mixed, grad_in, grad_up[None], grad_down[None])


def solution(mesh):
    placed = (
        P("dp", "tile"),
        P("dp", "tile"),
        P("tile", None, None, None),
        P("tile", None, None, None),
        P("tile", None),
        P("tile", None),
        P("tile"),
    )
    return jax.shard_map(
        body,
        mesh=mesh,
        in_specs=placed,
        out_specs=(
            P("dp", "tile"),
            P("dp", "tile"),
            P("tile", "dp", None, None),
            P("tile", "dp", None, None),
        ),
        check_vma=False,
    )
```

```python
import functools

import jax
import jax.numpy as jnp
from jax import lax
from jax.experimental import pallas as pl
from jax.experimental.pallas import tpu as pltpu
from jax.sharding import PartitionSpec as P

HIDDEN_SIZE = 16384
VMEM_LIMIT = 64 * 1024 * 1024 - 65536


def gelu_pair(pre):
    curve = lax.erf(pre * 0.7071067811865476)
    value = 0.5 * pre * (1.0 + curve)
    slope = 0.5 * (1.0 + curve) + pre * jnp.exp(-0.5 * pre * pre) * 0.3989422804014327
    return (value, slope)


NT = (((1,), (1,)), ((), ()))
TN = (((0,), (0,)), ((), ()))


def layer_kernel(n_dp, n_tile, slot_of, tokens, grad_out, up, down, x_all, hg_all, part,
                 xz, up_t, down_t, up_v, down_v, pre, hg, outbox, inbox,
                 own_sem, z_send, z_recv, f_send, f_recv, d_send, d_recv, l_send, l_recv, e_send, e_recv,
                 h_send, h_recv, m_send, m_recv, r_send, r_recv):
    n_z = n_tile // 2
    dp = lax.axis_index("dp")
    me = lax.axis_index("tile")
    z, core = me // 2, me % 2
    sib = 2 * z + (1 - core)
    feats = xz.shape[3]
    hidden = pre.shape[2]
    slots, side = up.shape[0], up.shape[1]
    block = min(256, hidden)
    pieces = hg.shape[0]
    piece = hg.shape[3]
    square = n_dp == 4
    if square:
        x_next = 2 * (dp // 2) + 1 - dp % 2
        y_next = 2 * (1 - dp // 2) + dp % 2
        across = n_dp - 1 - dp
        targets = sources = [x_next, y_next]
        arrivals = [x_next, y_next, across]
    else:
        targets = [(dp + k) % n_dp for k in range(1, n_dp)]
        sources = arrivals = [(dp + n_dp - k) % n_dp for k in range(1, n_dp)]
    direct = range(len(targets))

    def to(src, dst, ssem, rsem, d, t):
        return pltpu.make_async_remote_copy(
            src_ref=src, dst_ref=dst, send_sem=ssem, recv_sem=rsem,
            device_id={"dp": d, "tile": t}, device_id_type=pl.DeviceIdType.MESH)

    def owner(j):
        return 2 * ((z + n_z - j) % n_z) + core

    def other(j):
        return 2 * ((z + n_z - j) % n_z) + 1 - core

    def z_copy(j):
        return to(xz.at[me], xz.at[me], z_send.at[j], z_recv.at[j], dp, 2 * ((z + j) % n_z) + core)

    def f_copy(j):
        return to(xz.at[owner(j)], xz.at[owner(j)], f_send.at[j], f_recv.at[j], dp, sib)

    def d_copy(k, j):
        return to(xz.at[owner(j)], x_all.at[dp, owner(j)], d_send.at[k, j], d_recv.at[k, j], targets[k], me)

    def l_copy(k, j):
        slot = x_all.at[sources[k], owner(j), k]
        return to(slot, slot, l_send.at[k, j], l_recv.at[k, j], targets[1 - k], me)

    def e_copy(k, j):
        slot = x_all.at[arrivals[k], owner(j)]
        return to(slot, slot, e_send.at[k, j], e_recv.at[k, j], dp, sib)

    def h_copy(k, p):
        return to(hg.at[p], hg_all.at[dp, p], h_send.at[k, p], h_recv.at[k, p], targets[k], me)

    def m_copy(k, p):
        slot = hg_all.at[sources[k], p, k]
        return to(slot, slot, m_send.at[k, p], m_recv.at[k, p], targets[1 - k], me)

    def s_copy(j):
        return to(outbox.at[j], inbox.at[j], r_send.at[j], r_recv.at[j], dp, sib)

    def r_copy(j):
        i = n_z + j
        return to(outbox.at[i], inbox.at[i], r_send.at[i], r_recv.at[i], dp, 2 * ((z + j) % n_z) + core)

    def landed(j):
        for k in direct:
            d_copy(k, j).wait_recv()
            if square:
                l_copy(k, j).start()
            e_copy(k, j).start()

    barrier = pltpu.get_barrier_semaphore()
    for t in [sib] + [2 * ((z + j) % n_z) + core for j in range(1, n_z)]:
        pl.semaphore_signal(barrier, inc=1, device_id={"dp": dp, "tile": t},
                            device_id_type=pl.DeviceIdType.MESH)
    for k in direct:
        pl.semaphore_signal(barrier, inc=1, device_id={"dp": targets[k], "tile": me},
                            device_id_type=pl.DeviceIdType.MESH)
    own = [pltpu.make_async_copy(tokens, xz.at[me, 0], own_sem.at[0]),
           pltpu.make_async_copy(grad_out, xz.at[me, 1], own_sem.at[1])]
    load = [pltpu.make_async_copy(up, up_t.at[pl.ds(0, slots)], own_sem.at[2]),
            pltpu.make_async_copy(down, down_t.at[pl.ds(0, slots)], own_sem.at[3])]
    for copy in own + load:
        copy.start()
    up_t[slots] = jnp.zeros((side, side), up_t.dtype)
    down_t[slots] = jnp.zeros((side, side), down_t.dtype)
    pre[...] = jnp.zeros_like(pre)
    pl.semaphore_wait(barrier, n_z + len(targets))
    for copy in own:
        copy.wait()
    for j in range(1, n_z):
        z_copy(j).start()
    f_copy(0).start()
    for k in direct:
        d_copy(k, 0).start()
    for copy in load:
        copy.wait()

    def fill(t):
        wide = feats // side
        high = hidden // side

        @pl.loop(0, high)
        def _(r):
            at = pl.ds(pl.multiple_of(r * side, side), side)
            for c in range(wide):
                slot = slot_of[(t * wide + c) * high + r]
                up_v[t, c * side:(c + 1) * side, at] = up_t[slot]
                down_v[t, at, c * side:(c + 1) * side] = down_t[slot]

    def gather_in(t):
        @pl.loop(0, hidden // block)
        def _(b):
            at = pl.ds(pl.multiple_of(b * block, block), block)
            pre[0, :, at] += jnp.dot(xz[t, 0], up_v[t, :, at], preferred_element_type=jnp.float32)
            pre[1, :, at] += lax.dot_general(xz[t, 1], down_v[t, at, :], NT, preferred_element_type=jnp.float32)

    fill(owner(0))
    fill(other(0))
    for j in range(n_z):
        if j:
            z_copy(j).wait_recv()
            f_copy(j).start()
            for k in direct:
                d_copy(k, j).start()
        gather_in(owner(j))
        if j + 1 < n_z:
            fill(owner(j + 1))
            fill(other(j + 1))
        f_copy(j).wait_recv()
        gather_in(other(j))
        if j:
            landed(j - 1)

    for p in range(pieces):
        value, slope = gelu_pair(pre[0, :, p * piece:(p + 1) * piece])
        hg[p, 0] = value.astype(jnp.bfloat16)
        hg[p, 1] = (pre[1, :, p * piece:(p + 1) * piece] * slope).astype(jnp.bfloat16)
        for k in direct:
            h_copy(k, p).start()
    keep = [pltpu.make_async_copy(hg, hg_all.at[dp], own_sem.at[0]),
            pltpu.make_async_copy(xz, x_all.at[dp], own_sem.at[1])]
    for copy in keep:
        copy.start()

    def terms(t):
        out = jnp.zeros((pre.shape[1], feats), jnp.float32)
        back = jnp.zeros((pre.shape[1], feats), jnp.float32)
        for p in range(pieces):
            span = slice(p * piece, (p + 1) * piece)
            out += jnp.dot(hg[p, 0], down_v[t, span, :], preferred_element_type=jnp.float32)
            back += lax.dot_general(hg[p, 1], up_v[t, :, span], NT, preferred_element_type=jnp.float32)
        return out, back

    @pl.loop(0, n_z)
    def _(j):
        out, back = terms(2 * ((z + j) % n_z) + 1 - core)
        outbox[j, 0] = out.astype(jnp.bfloat16)
        outbox[j, 1] = back.astype(jnp.bfloat16)
        s_copy(j).start()

    def merged(j):
        out, back = terms(2 * ((z + j) % n_z) + core)
        s_copy(j).wait_recv()
        outbox[n_z + j, 0] = (out + inbox[j, 0].astype(jnp.float32)).astype(jnp.bfloat16)
        outbox[n_z + j, 1] = (back + inbox[j, 1].astype(jnp.float32)).astype(jnp.bfloat16)

    @pl.loop(1, n_z)
    def _(j):
        merged(j)
        r_copy(j).start()

    landed(n_z - 1)
    merged(0)
    def crossed(j):
        for k in direct:
            l_copy(k, j).wait_recv()
        e_copy(2, j).start()

    if square:
        for j in range(n_z - 1):
            crossed(j)
        for p in range(pieces):
            for k in direct:
                h_copy(k, p).wait_recv()
                m_copy(k, p).start()
            if p == pieces // 2:
                crossed(n_z - 1)
    for half in range(2):
        total = outbox[n_z, half].astype(jnp.float32)
        for j in range(1, n_z):
            if half == 0:
                r_copy(j).wait_recv()
            total = total + inbox[n_z + j, half].astype(jnp.float32)
        part[half] = total.astype(jnp.bfloat16)
    for copy in keep:
        copy.wait()
    for j in range(n_z):
        if j:
            z_copy(j).wait_send()
        f_copy(j).wait_send()
        for k in direct:
            d_copy(k, j).wait_send()
            if square:
                l_copy(k, j).wait_send()
        for k in range(n_dp - 1):
            e_copy(k, j).wait()
    for p in range(pieces):
        for k in direct:
            h_copy(k, p).wait_send()
            if square:
                m_copy(k, p).wait()
            else:
                h_copy(k, p).wait_recv()
    for j in range(n_z):
        s_copy(j).wait_send()
        if j:
            r_copy(j).wait_send()


def layer(slot_of, tokens, grad_out, up, down, n_dp, n_tile):
    count_tok, feats = tokens.shape
    slots, side = up.shape[:2]
    hidden = HIDDEN_SIZE // n_tile
    n_z = n_tile // 2
    pieces = min(4, hidden // side)
    hbm = pl.BlockSpec(memory_space=pl.ANY)
    vmem = pl.BlockSpec(memory_space=pltpu.VMEM)
    kind = jnp.bfloat16
    dma = pltpu.SemaphoreType.DMA
    box = pltpu.VMEM((n_tile, 2, count_tok, feats), kind)
    packed = (pieces, 2, count_tok, hidden // pieces)
    pairs = [dma((n_dp, n_z)), dma((n_dp, n_z))]
    sends = [dma((n_dp, pieces)), dma((n_dp, pieces))]
    return pl.pallas_call(
        functools.partial(layer_kernel, n_dp, n_tile),
        out_shape=(
            jax.ShapeDtypeStruct((n_dp, n_tile, 2, count_tok, feats), kind),
            jax.ShapeDtypeStruct((n_dp,) + packed, kind),
            jax.ShapeDtypeStruct((2,) + tokens.shape, kind),
        ),
        in_specs=[pl.BlockSpec(memory_space=pltpu.SMEM), hbm, hbm, hbm, hbm],
        out_specs=(hbm, hbm, vmem),
        scratch_shapes=[
            box,
            pltpu.VMEM((slots + 1, side, side), kind),
            pltpu.VMEM((slots + 1, side, side), kind),
            pltpu.VMEM((n_tile, feats, hidden), kind),
            pltpu.VMEM((n_tile, hidden, feats), kind),
            pltpu.VMEM((2, count_tok, hidden), jnp.float32),
            pltpu.VMEM(packed, kind),
            box,
            box,
            dma((4,)),
            dma((n_z,)),
            dma((n_z,)),
            dma((n_z,)),
            dma((n_z,)),
        ] + pairs * 3 + sends * 2 + [
            dma((n_tile,)),
            dma((n_tile,)),
        ],
        compiler_params=pltpu.CompilerParams(
            vmem_limit_bytes=VMEM_LIMIT, collective_id=0, has_side_effects=True
        ),
        name="layer",
    )(slot_of, tokens, grad_out, up, down)


def grads_kernel(scale, rows, cols, info, x, hg, part, grad_up, grad_down, mixed, grad_in):
    group, side = grad_up.shape[0], grad_up.shape[1]
    per = x.shape[4] // side
    wide = hg.shape[4] // side
    base = info[1] + pl.program_id(0) * group
    tokens = x.shape[0] * x.shape[3]

    @pl.when(pl.program_id(0) == 0)
    def _():
        mixed[...] = part[0]
        grad_in[...] = part[1]

    @pl.when(base < info[0])
    def _():
        for j in range(group):
            s = base + j
            owner = cols[s] // per
            f = pl.multiple_of((cols[s] - owner * per) * side, side)
            p = rows[s] // wide
            r = pl.multiple_of((rows[s] - p * wide) * side, side)
            xs = x[:, owner, 0, :, pl.ds(f, side)].reshape(tokens, side)
            dys = x[:, owner, 1, :, pl.ds(f, side)].reshape(tokens, side)
            h = hg[:, p, 0, :, pl.ds(r, side)].reshape(tokens, side)
            g = hg[:, p, 1, :, pl.ds(r, side)].reshape(tokens, side)
            up_sum = lax.dot_general(xs, g, TN, preferred_element_type=jnp.float32) * scale
            down_sum = lax.dot_general(h, dys, TN, preferred_element_type=jnp.float32) * scale
            grad_up[j] = jnp.where(s < info[0], up_sum, 0.0)
            grad_down[j] = jnp.where(s < info[0], down_sum, 0.0)

    @pl.when(base >= info[0])
    def _():
        grad_up[...] = jnp.zeros_like(grad_up)
        grad_down[...] = jnp.zeros_like(grad_down)


def grads(rows, cols, info, x, hg, part, slots, side, scale):
    smem = pl.BlockSpec(memory_space=pltpu.SMEM)
    group = min(8, slots)
    out = pl.BlockSpec((group, side, side), lambda i: (i, 0, 0))
    shape = jax.ShapeDtypeStruct((slots, side, side), jnp.float32)
    flat = jax.ShapeDtypeStruct(part.shape[1:], part.dtype)
    flat_spec = pl.BlockSpec(part.shape[1:], lambda i: (0, 0))
    return pl.pallas_call(
        functools.partial(grads_kernel, scale),
        grid=(slots // group,),
        out_shape=(shape, shape, flat, flat),
        in_specs=[
            smem,
            smem,
            smem,
            pl.BlockSpec(x.shape, lambda i: (0,) * 5, pipeline_mode=pl.Buffered(1)),
            pl.BlockSpec(hg.shape, lambda i: (0,) * 5, pipeline_mode=pl.Buffered(1)),
            pl.BlockSpec(part.shape, lambda i: (0,) * 3, pipeline_mode=pl.Buffered(1)),
        ],
        out_specs=(out, out, flat_spec, flat_spec),
        compiler_params=pltpu.CompilerParams(vmem_limit_bytes=VMEM_LIMIT),
        name="grads",
    )(rows, cols, info, x, hg, part)


def body(tokens, grad_out, up_tiles, down_tiles, tile_rows, tile_cols, tile_count):
    slots, side = up_tiles.shape[1:3]
    n_tile, n_dp = lax.axis_size("tile"), lax.axis_size("dp")
    high = HIDDEN_SIZE // (n_tile * side)
    cells = high * (tokens.shape[1] * n_tile // side)
    number = jnp.arange(slots, dtype=jnp.int32)
    place = jnp.where(number < tile_count[0], tile_cols[0] * high + tile_rows[0], -1)
    hit = place[None, :] == jnp.arange(cells, dtype=jnp.int32)[:, None]
    slot_of = jnp.min(jnp.where(hit, number[None, :], slots), axis=1)
    x_all, hg_all, part = layer(
        slot_of, tokens, grad_out, up_tiles[0], down_tiles[0], n_dp, n_tile
    )
    share = slots // n_dp
    info = jnp.concatenate([tile_count, (lax.axis_index("dp") * share).astype(jnp.int32)[None]])
    grad_up, grad_down, mixed, grad_in = grads(
        tile_rows[0], tile_cols[0], info, x_all, hg_all, part, share, side, 1.0 / n_dp
    )
    return (mixed, grad_in, grad_up[None], grad_down[None])


def solution(mesh):
    placed = (
        P("dp", "tile"),
        P("dp", "tile"),
        P("tile", None, None, None),
        P("tile", None, None, None),
        P("tile", None),
        P("tile", None),
        P("tile"),
    )
    return jax.shard_map(
        body,
        mesh=mesh,
        in_specs=placed,
        out_specs=(
            P("dp", "tile"),
            P("dp", "tile"),
            P("tile", "dp", None, None),
            P("tile", "dp", None, None),
        ),
        check_vma=False,
    )
```

```python
import functools

import jax
import jax.numpy as jnp
from jax import lax
from jax.experimental import pallas as pl
from jax.experimental.pallas import tpu as pltpu
from jax.sharding import PartitionSpec as P

HIDDEN_SIZE = 16384
VMEM_LIMIT = 64 * 1024 * 1024 - 65536


def gelu_pair(pre):
    curve = lax.erf(pre * 0.7071067811865476)
    value = 0.5 * pre * (1.0 + curve)
    slope = 0.5 * (1.0 + curve) + pre * jnp.exp(-0.5 * pre * pre) * 0.3989422804014327
    return (value, slope)


NT = (((1,), (1,)), ((), ()))
TN = (((0,), (0,)), ((), ()))


def layer_kernel(n_dp, n_tile, slot_of, tokens, grad_out, up, down, x_all, hg_all, part,
                 xz, up_t, down_t, up_v, down_v, pre, hg, outbox, inbox,
                 own_sem, z_send, z_recv, f_send, f_recv, d_send, d_recv, l_send, l_recv, e_send, e_recv,
                 h_send, h_recv, m_send, m_recv, r_send, r_recv):
    n_z = n_tile // 2
    dp = lax.axis_index("dp")
    me = lax.axis_index("tile")
    z, core = me // 2, me % 2
    sib = 2 * z + (1 - core)
    feats = xz.shape[3]
    hidden = pre.shape[2]
    slots, side = up.shape[0], up.shape[1]
    block = min(256, hidden)
    pieces = hg.shape[0]
    piece = hg.shape[3]
    square = n_dp == 4
    if square:
        x_next = 2 * (dp // 2) + 1 - dp % 2
        y_next = 2 * (1 - dp // 2) + dp % 2
        across = n_dp - 1 - dp
        targets = sources = [x_next, y_next]
        arrivals = [x_next, y_next, across]
    else:
        targets = [(dp + k) % n_dp for k in range(1, n_dp)]
        sources = arrivals = [(dp + n_dp - k) % n_dp for k in range(1, n_dp)]
    direct = range(len(targets))

    def to(src, dst, ssem, rsem, d, t):
        return pltpu.make_async_remote_copy(
            src_ref=src, dst_ref=dst, send_sem=ssem, recv_sem=rsem,
            device_id={"dp": d, "tile": t}, device_id_type=pl.DeviceIdType.MESH)

    def owner(j):
        return 2 * ((z + n_z - j) % n_z) + core

    def other(j):
        return 2 * ((z + n_z - j) % n_z) + 1 - core

    def z_copy(j):
        return to(xz.at[me], xz.at[me], z_send.at[j], z_recv.at[j], dp, 2 * ((z + j) % n_z) + core)

    def f_copy(j):
        return to(xz.at[owner(j)], xz.at[owner(j)], f_send.at[j], f_recv.at[j], dp, sib)

    def d_copy(k, j):
        return to(xz.at[owner(j)], x_all.at[dp, owner(j)], d_send.at[k, j], d_recv.at[k, j], targets[k], me)

    def l_copy(k, j):
        slot = x_all.at[sources[k], owner(j), k]
        return to(slot, slot, l_send.at[k, j], l_recv.at[k, j], targets[1 - k], me)

    def e_copy(k, j):
        slot = x_all.at[arrivals[k], owner(j)]
        return to(slot, slot, e_send.at[k, j], e_recv.at[k, j], dp, sib)

    def h_copy(k, p):
        return to(hg.at[p], hg_all.at[dp, p], h_send.at[k, p], h_recv.at[k, p], targets[k], me)

    def m_copy(k, p):
        slot = hg_all.at[sources[k], p, k]
        return to(slot, slot, m_send.at[k, p], m_recv.at[k, p], targets[1 - k], me)

    def s_copy(j):
        return to(outbox.at[j], inbox.at[j], r_send.at[j], r_recv.at[j], dp, sib)

    def r_copy(j):
        i = n_z + j
        return to(outbox.at[i], inbox.at[i], r_send.at[i], r_recv.at[i], dp, 2 * ((z + j) % n_z) + core)

    def landed(j):
        for k in direct:
            d_copy(k, j).wait_recv()
            if square:
                l_copy(k, j).start()
            e_copy(k, j).start()

    barrier = pltpu.get_barrier_semaphore()
    for t in [sib] + [2 * ((z + j) % n_z) + core for j in range(1, n_z)]:
        pl.semaphore_signal(barrier, inc=1, device_id={"dp": dp, "tile": t},
                            device_id_type=pl.DeviceIdType.MESH)
    for k in direct:
        pl.semaphore_signal(barrier, inc=1, device_id={"dp": targets[k], "tile": me},
                            device_id_type=pl.DeviceIdType.MESH)
    own = [pltpu.make_async_copy(tokens, xz.at[me, 0], own_sem.at[0]),
           pltpu.make_async_copy(grad_out, xz.at[me, 1], own_sem.at[1])]
    load = [pltpu.make_async_copy(up, up_t.at[pl.ds(0, slots)], own_sem.at[2]),
            pltpu.make_async_copy(down, down_t.at[pl.ds(0, slots)], own_sem.at[3])]
    for copy in own + load:
        copy.start()
    up_t[slots] = jnp.zeros((side, side), up_t.dtype)
    down_t[slots] = jnp.zeros((side, side), down_t.dtype)
    pre[...] = jnp.zeros_like(pre)
    pl.semaphore_wait(barrier, n_z + len(targets))
    for copy in own:
        copy.wait()
    for j in range(1, n_z):
        z_copy(j).start()
    f_copy(0).start()
    for k in direct:
        d_copy(k, 0).start()
    for copy in load:
        copy.wait()

    def fill(t):
        wide = feats // side
        high = hidden // side

        @pl.loop(0, high)
        def _(r):
            at = pl.ds(pl.multiple_of(r * side, side), side)
            for c in range(wide):
                slot = slot_of[(t * wide + c) * high + r]
                up_v[t, c * side:(c + 1) * side, at] = up_t[slot]
                down_v[t, at, c * side:(c + 1) * side] = down_t[slot]

    def gather_in(t):
        @pl.loop(0, hidden // block)
        def _(b):
            at = pl.ds(pl.multiple_of(b * block, block), block)
            pre[0, :, at] += jnp.dot(xz[t, 0], up_v[t, :, at], preferred_element_type=jnp.float32)
            pre[1, :, at] += lax.dot_general(xz[t, 1], down_v[t, at, :], NT, preferred_element_type=jnp.float32)

    fill(owner(0))
    fill(other(0))
    for j in range(n_z):
        if j:
            z_copy(j).wait_recv()
            f_copy(j).start()
            for k in direct:
                d_copy(k, j).start()
        gather_in(owner(j))
        if j + 1 < n_z:
            fill(owner(j + 1))
            fill(other(j + 1))
        f_copy(j).wait_recv()
        gather_in(other(j))
        if j:
            landed(j - 1)

    for p in range(pieces):
        value, slope = gelu_pair(pre[0, :, p * piece:(p + 1) * piece])
        hg[p, 0] = value.astype(jnp.bfloat16)
        hg[p, 1] = (pre[1, :, p * piece:(p + 1) * piece] * slope).astype(jnp.bfloat16)
        for k in direct:
            h_copy(k, p).start()
    keep = [pltpu.make_async_copy(hg, hg_all.at[dp], own_sem.at[0]),
            pltpu.make_async_copy(xz, x_all.at[dp], own_sem.at[1])]
    for copy in keep:
        copy.start()

    def terms(t):
        out = jnp.zeros((pre.shape[1], feats), jnp.float32)
        back = jnp.zeros((pre.shape[1], feats), jnp.float32)
        for p in range(pieces):
            span = slice(p * piece, (p + 1) * piece)
            out += jnp.dot(hg[p, 0], down_v[t, span, :], preferred_element_type=jnp.float32)
            back += lax.dot_general(hg[p, 1], up_v[t, :, span], NT, preferred_element_type=jnp.float32)
        return out, back

    @pl.loop(0, n_z)
    def _(j):
        out, back = terms(2 * ((z + j) % n_z) + 1 - core)
        outbox[j, 0] = out.astype(jnp.bfloat16)
        outbox[j, 1] = back.astype(jnp.bfloat16)
        s_copy(j).start()

    def merged(j):
        out, back = terms(2 * ((z + j) % n_z) + core)
        s_copy(j).wait_recv()
        outbox[n_z + j, 0] = (out + inbox[j, 0].astype(jnp.float32)).astype(jnp.bfloat16)
        outbox[n_z + j, 1] = (back + inbox[j, 1].astype(jnp.float32)).astype(jnp.bfloat16)

    landed(n_z - 1)

    @pl.loop(1, n_z)
    def _(j):
        merged(j)
        r_copy(j).start()

    merged(0)
    def crossed(j):
        for k in direct:
            l_copy(k, j).wait_recv()
        e_copy(2, j).start()

    if square:
        for j in range(n_z - 1):
            crossed(j)
        for p in range(pieces):
            for k in direct:
                h_copy(k, p).wait_recv()
                m_copy(k, p).start()
            if p == pieces // 2:
                crossed(n_z - 1)
    for half in range(2):
        total = outbox[n_z, half].astype(jnp.float32)
        for j in range(1, n_z):
            if half == 0:
                r_copy(j).wait_recv()
            total = total + inbox[n_z + j, half].astype(jnp.float32)
        part[half] = total.astype(jnp.bfloat16)
    for copy in keep:
        copy.wait()
    for j in range(n_z):
        if j:
            z_copy(j).wait_send()
        f_copy(j).wait_send()
        for k in direct:
            d_copy(k, j).wait_send()
            if square:
                l_copy(k, j).wait_send()
        for k in range(n_dp - 1):
            e_copy(k, j).wait()
    for p in range(pieces):
        for k in direct:
            h_copy(k, p).wait_send()
            if square:
                m_copy(k, p).wait()
            else:
                h_copy(k, p).wait_recv()
    for j in range(n_z):
        s_copy(j).wait_send()
        if j:
            r_copy(j).wait_send()


def layer(slot_of, tokens, grad_out, up, down, n_dp, n_tile):
    count_tok, feats = tokens.shape
    slots, side = up.shape[:2]
    hidden = HIDDEN_SIZE // n_tile
    n_z = n_tile // 2
    pieces = min(4, hidden // side)
    hbm = pl.BlockSpec(memory_space=pl.ANY)
    vmem = pl.BlockSpec(memory_space=pltpu.VMEM)
    kind = jnp.bfloat16
    dma = pltpu.SemaphoreType.DMA
    box = pltpu.VMEM((n_tile, 2, count_tok, feats), kind)
    packed = (pieces, 2, count_tok, hidden // pieces)
    pairs = [dma((n_dp, n_z)), dma((n_dp, n_z))]
    sends = [dma((n_dp, pieces)), dma((n_dp, pieces))]
    return pl.pallas_call(
        functools.partial(layer_kernel, n_dp, n_tile),
        out_shape=(
            jax.ShapeDtypeStruct((n_dp, n_tile, 2, count_tok, feats), kind),
            jax.ShapeDtypeStruct((n_dp,) + packed, kind),
            jax.ShapeDtypeStruct((2,) + tokens.shape, kind),
        ),
        in_specs=[pl.BlockSpec(memory_space=pltpu.SMEM), hbm, hbm, hbm, hbm],
        out_specs=(hbm, hbm, vmem),
        scratch_shapes=[
            box,
            pltpu.VMEM((slots + 1, side, side), kind),
            pltpu.VMEM((slots + 1, side, side), kind),
            pltpu.VMEM((n_tile, feats, hidden), kind),
            pltpu.VMEM((n_tile, hidden, feats), kind),
            pltpu.VMEM((2, count_tok, hidden), jnp.float32),
            pltpu.VMEM(packed, kind),
            box,
            box,
            dma((4,)),
            dma((n_z,)),
            dma((n_z,)),
            dma((n_z,)),
            dma((n_z,)),
        ] + pairs * 3 + sends * 2 + [
            dma((n_tile,)),
            dma((n_tile,)),
        ],
        compiler_params=pltpu.CompilerParams(
            vmem_limit_bytes=VMEM_LIMIT, collective_id=0, has_side_effects=True
        ),
        name="layer",
    )(slot_of, tokens, grad_out, up, down)


def grads_kernel(scale, rows, cols, info, x, hg, part, grad_up, grad_down, mixed, grad_in):
    group, side = grad_up.shape[0], grad_up.shape[1]
    per = x.shape[4] // side
    wide = hg.shape[4] // side
    base = info[1] + pl.program_id(0) * group
    tokens = x.shape[0] * x.shape[3]

    @pl.when(pl.program_id(0) == 0)
    def _():
        mixed[...] = part[0]
        grad_in[...] = part[1]

    @pl.when(base < info[0])
    def _():
        for j in range(group):
            s = base + j
            owner = cols[s] // per
            f = pl.multiple_of((cols[s] - owner * per) * side, side)
            p = rows[s] // wide
            r = pl.multiple_of((rows[s] - p * wide) * side, side)
            xs = x[:, owner, 0, :, pl.ds(f, side)].reshape(tokens, side)
            dys = x[:, owner, 1, :, pl.ds(f, side)].reshape(tokens, side)
            h = hg[:, p, 0, :, pl.ds(r, side)].reshape(tokens, side)
            g = hg[:, p, 1, :, pl.ds(r, side)].reshape(tokens, side)
            up_sum = lax.dot_general(xs, g, TN, preferred_element_type=jnp.float32) * scale
            down_sum = lax.dot_general(h, dys, TN, preferred_element_type=jnp.float32) * scale
            grad_up[j] = jnp.where(s < info[0], up_sum, 0.0)
            grad_down[j] = jnp.where(s < info[0], down_sum, 0.0)

    @pl.when(base >= info[0])
    def _():
        grad_up[...] = jnp.zeros_like(grad_up)
        grad_down[...] = jnp.zeros_like(grad_down)


def grads(rows, cols, info, x, hg, part, slots, side, scale):
    smem = pl.BlockSpec(memory_space=pltpu.SMEM)
    group = min(8, slots)
    out = pl.BlockSpec((group, side, side), lambda i: (i, 0, 0))
    shape = jax.ShapeDtypeStruct((slots, side, side), jnp.float32)
    flat = jax.ShapeDtypeStruct(part.shape[1:], part.dtype)
    flat_spec = pl.BlockSpec(part.shape[1:], lambda i: (0, 0))
    return pl.pallas_call(
        functools.partial(grads_kernel, scale),
        grid=(slots // group,),
        out_shape=(shape, shape, flat, flat),
        in_specs=[
            smem,
            smem,
            smem,
            pl.BlockSpec(x.shape, lambda i: (0,) * 5, pipeline_mode=pl.Buffered(1)),
            pl.BlockSpec(hg.shape, lambda i: (0,) * 5, pipeline_mode=pl.Buffered(1)),
            pl.BlockSpec(part.shape, lambda i: (0,) * 3, pipeline_mode=pl.Buffered(1)),
        ],
        out_specs=(out, out, flat_spec, flat_spec),
        compiler_params=pltpu.CompilerParams(vmem_limit_bytes=VMEM_LIMIT),
        name="grads",
    )(rows, cols, info, x, hg, part)


def body(tokens, grad_out, up_tiles, down_tiles, tile_rows, tile_cols, tile_count):
    slots, side = up_tiles.shape[1:3]
    n_tile, n_dp = lax.axis_size("tile"), lax.axis_size("dp")
    high = HIDDEN_SIZE // (n_tile * side)
    cells = high * (tokens.shape[1] * n_tile // side)
    number = jnp.arange(slots, dtype=jnp.int32)
    place = jnp.where(number < tile_count[0], tile_cols[0] * high + tile_rows[0], -1)
    hit = place[None, :] == jnp.arange(cells, dtype=jnp.int32)[:, None]
    slot_of = jnp.min(jnp.where(hit, number[None, :], slots), axis=1)
    x_all, hg_all, part = layer(
        slot_of, tokens, grad_out, up_tiles[0], down_tiles[0], n_dp, n_tile
    )
    share = slots // n_dp
    info = jnp.concatenate([tile_count, (lax.axis_index("dp") * share).astype(jnp.int32)[None]])
    grad_up, grad_down, mixed, grad_in = grads(
        tile_rows[0], tile_cols[0], info, x_all, hg_all, part, share, side, 1.0 / n_dp
    )
    return (mixed, grad_in, grad_up[None], grad_down[None])


def solution(mesh):
    placed = (
        P("dp", "tile"),
        P("dp", "tile"),
        P("tile", None, None, None),
        P("tile", None, None, None),
        P("tile", None),
        P("tile", None),
        P("tile"),
    )
    return jax.shard_map(
        body,
        mesh=mesh,
        in_specs=placed,
        out_specs=(
            P("dp", "tile"),
            P("dp", "tile"),
            P("tile", "dp", None, None),
            P("tile", "dp", None, None),
        ),
        check_vma=False,
    )
```
